1024 devices in a mesh: pipe: 4 (over y_lo, core), dp: 4 (over y_hi), ctx: 64 (over z, x).
Axes of the slice: x: 4, y: 8 (y_hi: 4, y_lo: 2; y = y_hi * 2 + y_lo), z: 16, core: 2. Of those that a mesh axis runs over, the one named last changes fastest.
Arguments:
- projected: bfloat16 [3, 4, 65536, 1536], P(None, 'pipe', ('dp', 'ctx')), parts along dimension 2, may hold values from -6 to 6, as said below
- tile_mask: int32 [256, 9], P('ctx'), may hold values from 0 to 1, as said below
Outputs:
- attended: bfloat16 [4, 65536, 1536], P('pipe', ('dp', 'ctx')), parts along dimension 1
The draws below stay inside these ranges and needn't reach their ends.
There are 4 independent parts, one for each index of `dp`. The reference program is written for one: setup_inputs(seed, part) draws one part's arguments, and reference() takes and returns one part's arrays. A program takes and returns all parts, laid end to end along the dimension named above; an argument that names none is the same for every part. Nothing has to cross between parts.
Inputs may be any that keep to these rules, and one draw needn't show every extreme that they name: `projected`: queries, keys and values of the heads, stacked. `tile_mask`: 0 or 1; entry [t, 4] is 1 for every tile t.
All inputs are finite; a program needn't handle non-finite values.
Results may differ from the reference program's by a relative error of at most 0.0045.
Values may be sent and summed in bfloat16 or wider, within the bound.
No kernel may reach another device: no remote copies, remote signals or barrier semaphores. Data moves between devices by JAX's collectives and lax.ppermute only.
A program may use at most 32 MiB of HBM per device.

```python
import math
import jax
import jax.numpy as jnp
from jax import lax

HEAD_DIM = 128
TILE = 64
REACH = 4
TILES_DEV = 4
ROWS_DEV = 256
TOKENS = 16384
TILES = 256
HD = 1536
N_PIPE = 4
N_CTX = 64


def draw_projected(key, part):
    shape = (3, N_PIPE, TOKENS, HD)
    stacked = jnp.clip(jax.random.normal(jax.random.fold_in(key, 103), shape, jnp.float32), -4.0, 4.0)
    return stacked.astype(jnp.bfloat16)


def draw_tile_mask(key, part):
    picks = jax.random.randint(jax.random.fold_in(key, 201), (TILES, 2 * REACH + 1), 0, 2)
    column = jax.lax.broadcasted_iota(jnp.int32, (TILES, 2 * REACH + 1), 1)
    return jnp.where(column == REACH, 1, picks).astype(jnp.int32)


def setup_inputs(seed: int = 0, part: int = 0) -> dict:
    keys = jax.random.split(jax.random.key(seed), 3)
    part_keys = jax.random.split(jax.random.fold_in(keys[2], part), 3)
    return {
        "projected": draw_projected(jax.random.fold_in(jax.random.fold_in(keys[2], part), 71), part),
        "tile_mask": draw_tile_mask(jax.random.fold_in(keys[2], 71), part),
    }


def admitted(tile_mask, block_index, tiles_dev, total_tiles):
    span_tiles = tiles_dev + 2 * REACH
    query_tile = jnp.arange(tiles_dev, dtype=jnp.int32)[:, None, None]
    key_tile = jnp.arange(span_tiles, dtype=jnp.int32)[None, :, None]
    offset_idx = jnp.arange(2 * REACH + 1, dtype=jnp.int32)[None, None, :]
    matches = (key_tile - query_tile == offset_idx) & (tile_mask[:, None, :] == 1)
    tiles_ok = jnp.any(matches, axis=-1)
    global_tile = block_index * tiles_dev + jnp.arange(span_tiles, dtype=jnp.int32) - REACH
    inside = (global_tile >= 0) & (global_tile < total_tiles)
    tiles_ok = tiles_ok & inside[None, :]
    return jnp.repeat(jnp.repeat(tiles_ok, TILE, axis=0), TILE, axis=1)

def attend(query_rows, key_rows, value_rows, allowed):
    query_count = query_rows.shape[0]
    span_len = key_rows.shape[0]
    head_count = query_rows.shape[1] // HEAD_DIM
    query_heads = query_rows.reshape(query_count, head_count, HEAD_DIM).astype(jnp.float32)
    key_heads = key_rows.reshape(span_len, head_count, HEAD_DIM).astype(jnp.float32)
    value_heads = value_rows.reshape(span_len, head_count, HEAD_DIM).astype(jnp.float32)
    score_scale = 1.0 / math.sqrt(HEAD_DIM)
    scores = jnp.einsum('qhd,khd->hqk', query_heads, key_heads) * score_scale
    scores = jnp.where(allowed[None], scores, -jnp.inf)
    row_max = lax.optimization_barrier(jnp.max(scores, axis=-1, keepdims=True))
    weights = lax.optimization_barrier(jnp.exp(scores - row_max).astype(jnp.bfloat16)).astype(jnp.float32)
    denominator = lax.optimization_barrier(jnp.sum(weights, axis=-1))
    numerator = jnp.einsum('hqk,khd->qhd', weights, value_heads)
    result = numerator / jnp.transpose(denominator)[:, :, None]
    return result.astype(jnp.bfloat16).reshape(query_count, head_count * HEAD_DIM)

def reference(projected, tile_mask):
    source = jnp.roll(projected, 1, axis=1)
    rim_width = REACH * TILE
    padded = jnp.pad(source[1:], ((0, 0), (0, 0), (rim_width, rim_width), (0, 0)))
    zero = jnp.zeros((), jnp.int32)

    def one_block(position):
        section_index = (position // N_CTX).astype(jnp.int32)
        block_index = (position % N_CTX).astype(jnp.int32)
        query_rows = lax.dynamic_slice(source[0], (section_index, block_index * ROWS_DEV, zero), (1, ROWS_DEV, HD))[0]
        key_values = lax.dynamic_slice(padded, (zero, section_index, block_index * ROWS_DEV, zero), (2, 1, ROWS_DEV + 2 * rim_width, HD))
        mask_rows = lax.dynamic_slice(tile_mask, (block_index * TILES_DEV, zero), (TILES_DEV, 2 * REACH + 1))
        allowed = admitted(mask_rows, block_index, TILES_DEV, TILES)
        return attend(query_rows, key_values[0, 0], key_values[1, 0], allowed)
    blocks = lax.map(one_block, jnp.arange(N_PIPE * N_CTX, dtype=jnp.int32))
    return blocks.reshape(N_PIPE, TOKENS, HD)
```

```python
import functools
import math

import jax
import jax.numpy as jnp
from jax import lax
from jax.experimental import pallas as pl
from jax.experimental.pallas import tpu as pltpu
from jax.sharding import PartitionSpec as P

HEAD_DIM = 128
TILE = 64
REACH = 4
SPAN = 640
EARLY = ((0, 4), (4, 8))
LATE = ((8, 10), (10, 12))


def columns(heads):
    return slice(heads[0] * HEAD_DIM, heads[1] * HEAD_DIM)


def ring(axis):
    count = lax.axis_size(axis)
    return [(i, (i + 1) % count) for i in range(count)]


def halo(cells):
    ends = lax.axis_size("ctx") - 1
    from_left = lax.ppermute(cells, "ctx", [(i, i + 1) for i in range(ends)])
    from_right = lax.ppermute(cells, "ctx", [(i + 1, i) for i in range(ends)])
    return from_left, from_right


def attend_heads(mask_ref, own_ref, left_ref, right_ref, store, heads):
    block_index = lax.axis_index("ctx")
    total_tiles = lax.axis_size("ctx") * 4
    scale = math.log2(math.e) / math.sqrt(HEAD_DIM)
    lane = lax.broadcasted_iota(jnp.int32, (1, 128), 1)
    zero, never = jnp.float32(0.0), jnp.float32(-jnp.inf)

    def penalty(t, s):
        c = s - t
        if c < 0 or c > 2 * REACH:
            return never
        tile = block_index * 4 + s - REACH
        ok = (mask_ref[t, c] == 1) & (tile >= 0) & (tile < total_tiles)
        return jnp.where(ok, zero, never)

    bias = []
    for t in range(4):
        first = 2 * (t // 2)
        bias.append(
            jnp.concatenate(
                [
                    jnp.where(lane < TILE, penalty(t, first + 2 * j), penalty(t, first + 2 * j + 1))
                    for j in range(5)
                ],
                axis=1,
            )
        )

    dims = (((1,), (1,)), ((), ()))
    for h in range(heads):
        cols = slice(h * HEAD_DIM, (h + 1) * HEAD_DIM)
        q = own_ref[0, 0, :, cols]
        keys = (left_ref[0, :, cols], own_ref[1, 0, :, cols], right_ref[0, :, cols])
        values = (left_ref[1, :, cols], own_ref[2, 0, :, cols], right_ref[1, :, cols])
        scores = [lax.dot_general(q, k, dims, preferred_element_type=jnp.float32) for k in keys]
        weights = [[], [], []]
        sums = []
        for t in range(4):
            rows = slice(t * TILE, (t + 1) * TILE)
            cut = 128 * (t // 2)
            x = jnp.concatenate(
                [scores[0][rows, cut:], scores[1][rows], scores[2][rows, : cut + 128]], axis=1
            )
            x = x * scale + bias[t]
            top = jnp.max(x, axis=1, keepdims=True)
            w = jnp.exp2(x - top).astype(jnp.bfloat16)
            sums.append(jnp.sum(w.astype(jnp.float32), axis=1, keepdims=True))
            pad = jnp.zeros((TILE, 128), jnp.bfloat16)
            if cut:
                weights[0].append(jnp.concatenate([pad, w[:, :128]], axis=1))
                weights[1].append(w[:, 128:384])
                weights[2].append(w[:, 384:])
            else:
                weights[0].append(w[:, :256])
                weights[1].append(w[:, 256:512])
                weights[2].append(jnp.concatenate([w[:, 512:], pad], axis=1))
        total = sum(
            jnp.dot(jnp.concatenate(w, axis=0), v, preferred_element_type=jnp.float32)
            for w, v in zip(weights, values)
        )
        denominator = jnp.concatenate(sums, axis=0)
        store(cols, (total * (1.0 / denominator)).astype(jnp.bfloat16))


def chunk_kernel(heads, mask_ref, own_ref, left_ref, right_ref, out_ref):
    def store(cols, value):
        out_ref[:, cols] = value

    attend_heads(mask_ref, own_ref, left_ref, right_ref, store, heads)


def last_kernel(heads, mask_ref, own_ref, left_ref, right_ref, _, out_ref):
    def store(cols, value):
        out_ref[0, :, cols] = value

    attend_heads(mask_ref, own_ref, left_ref, right_ref, store, heads)


def cost(heads, rows):
    return pl.CostEstimate(
        flops=4 * heads * rows * 3 * rows * HEAD_DIM,
        bytes_accessed=2 * 8 * heads * rows * HEAD_DIM,
        transcendentals=heads * rows * SPAN,
    )


def attend_chunk(mask, own, left, right, own_block, buffer=None, out_block=0):
    _, rows, width = left.shape
    heads = width // HEAD_DIM
    specs = [
        pl.BlockSpec(memory_space=pltpu.SMEM),
        pl.BlockSpec((3, 1, rows, width), lambda i: (0, 0, 0, own_block)),
        pl.BlockSpec((2, rows, width), lambda i: (0, 0, 0)),
        pl.BlockSpec((2, rows, width), lambda i: (0, 0, 0)),
    ]
    if buffer is None:
        return pl.pallas_call(
            functools.partial(chunk_kernel, heads),
            grid=(1,),
            out_shape=jax.ShapeDtypeStruct((rows, width), jnp.bfloat16),
            in_specs=specs,
            out_specs=pl.BlockSpec((rows, width), lambda i: (0, 0)),
            cost_estimate=cost(heads, rows),
            name="attend",
        )(mask, own, left, right)
    return pl.pallas_call(
        functools.partial(last_kernel, heads),
        grid=(1,),
        out_shape=jax.ShapeDtypeStruct(buffer.shape, buffer.dtype),
        in_specs=specs + [pl.BlockSpec(memory_space=pl.ANY)],
        out_specs=pl.BlockSpec((1, rows, width), lambda i: (0, 0, out_block)),
        input_output_aliases={4: 0},
        cost_estimate=cost(heads, rows),
        name="attend_last",
    )(mask, own, left, right, buffer)


def gather_kernel(spots, *refs):
    out_ref = refs[-1]
    for ref, cols in zip(refs[:-1], spots):
        out_ref[0, :, cols] = ref[...]


def gather(pieces, spots, shape):
    return pl.pallas_call(
        functools.partial(gather_kernel, spots),
        grid=(1,),
        out_shape=jax.ShapeDtypeStruct(shape, jnp.bfloat16),
        in_specs=[pl.BlockSpec(p.shape, lambda i: (0, 0)) for p in pieces],
        out_specs=pl.BlockSpec(shape, lambda i: (0, 0, 0)),
        name="gather",
    )(*pieces)


def shards(projected, tile_mask):
    _, _, rows, width = projected.shape
    early = [halo(projected[1:, 0, :, columns(c)]) for c in EARLY]
    span = slice(columns(LATE[0]).start, columns(LATE[-1]).stop)
    moved = lax.ppermute(projected[:, :, :, span], "pipe", ring("pipe"))
    late = []
    for c in LATE:
        cols = columns(c)
        late.append(halo(moved[1:, 0, :, cols.start - span.start : cols.stop - span.start]))
    pieces, spots = [], []
    for c, (left, right) in zip(EARLY, early):
        cols = columns(c)
        out = attend_chunk(tile_mask, projected, left, right, cols.start // (cols.stop - cols.start))
        pieces.append(lax.ppermute(out, "pipe", ring("pipe")))
        spots.append(cols)
    for n, (c, (left, right)) in enumerate(zip(LATE, late)):
        cols = columns(c)
        wide = cols.stop - cols.start
        block = (cols.start - span.start) // wide
        if n < len(LATE) - 1:
            pieces.append(attend_chunk(tile_mask, moved, left, right, block))
            spots.append(cols)
        else:
            buffer = gather(pieces, spots, (1, rows, width))
            return attend_chunk(tile_mask, moved, left, right, block, buffer, cols.start // wide)


def solution(mesh):
    placed = (P(None, "pipe", ("dp", "ctx"), None), P("ctx", None))
    return jax.shard_map(
        shards,
        mesh=mesh,
        in_specs=placed,
        out_specs=P("pipe", ("dp", "ctx"), None),
        check_vma=False,
    )
```

```python
import functools
import math

import jax
import jax.numpy as jnp
from jax import lax
from jax.experimental import pallas as pl
from jax.experimental.pallas import tpu as pltpu
from jax.sharding import PartitionSpec as P


HEAD_DIM = 128
TILE = 64
REACH = 4
SPAN = 640
EARLY = (((0, 6),), ((6, 9),))
LATE = ((9, 12),)

VMEM = pl.BlockSpec(memory_space=pltpu.VMEM)
GRANT = 16 << 20


def columns(heads, base=0):
    return slice((heads[0] - base) * HEAD_DIM, (heads[1] - base) * HEAD_DIM)


def ring(axis):
    count = lax.axis_size(axis)
    return [(i, (i + 1) % count) for i in range(count)]


def swap(cells, first):
    count = lax.axis_size("ctx")
    pairs = []
    for i in range(first, count - 1, 2):
        pairs += [(i, i + 1), (i + 1, i)]
    return lax.ppermute(cells, "ctx", pairs)


def bias_kernel(mask_ref, out_ref):
    block_index = lax.axis_index("ctx")
    total_tiles = lax.axis_size("ctx") * 4
    lane = lax.broadcasted_iota(jnp.int32, (8, 128), 1)
    zero, never = jnp.float32(0.0), jnp.float32(-jnp.inf)

    def penalty(t, s):
        c = s - t
        if c < 0 or c > 2 * REACH:
            return never
        tile = block_index * 4 + s - REACH
        ok = (mask_ref[t, c] == 1) & (tile >= 0) & (tile < total_tiles)
        return jnp.where(ok, zero, never)

    for t in range(4):
        first = 2 * (t // 2)
        for j in range(5):
            row = jnp.where(lane < TILE, penalty(t, first + 2 * j), penalty(t, first + 2 * j + 1))
            out_ref[t, :, j * 128 : (j + 1) * 128] = row


def bias_of(mask):
    return pl.pallas_call(
        bias_kernel,
        out_shape=jax.ShapeDtypeStruct((4, 8, SPAN), jnp.float32),
        in_specs=[pl.BlockSpec(memory_space=pltpu.SMEM)],
        out_specs=VMEM,
        compiler_params=pltpu.CompilerParams(vmem_limit_bytes=GRANT),
        name="bias",
    )(mask)


def attend_heads(bias_ref, own, left, right, store, heads):
    scale = math.log2(math.e) / math.sqrt(HEAD_DIM)
    dims = (((1,), (1,)), ((), ()))

    def scores_of(h):
        q = own(0, h)
        keys = (left(0, h), own(1, h), right(0, h))
        return [lax.dot_general(q, k, dims, preferred_element_type=jnp.float32) for k in keys]

    def weights_of(scores):
        weights = [[], [], []]
        for t in range(4):
            rows = slice(t * TILE, (t + 1) * TILE)
            cut = 128 * (t // 2)
            x = jnp.concatenate(
                [scores[0][rows, cut:], scores[1][rows], scores[2][rows, : cut + 128]], axis=1
            )
            x = (x.reshape(8, 8, SPAN) * scale + bias_ref[t][None]).reshape(TILE, SPAN)
            top = jnp.max(x, axis=1, keepdims=True)
            w = jnp.exp2(x - top).astype(jnp.bfloat16)
            pad = jnp.zeros((TILE, 128), jnp.bfloat16)
            if cut:
                weights[0].append(jnp.concatenate([pad, w[:, :128]], axis=1))
                weights[1].append(w[:, 128:384])
                weights[2].append(w[:, 384:])
            else:
                weights[0].append(w[:, :256])
                weights[1].append(w[:, 256:512])
                weights[2].append(jnp.concatenate([w[:, 512:], pad], axis=1))
        return [jnp.concatenate(w, axis=0) for w in weights]

    ones = jnp.ones((256, HEAD_DIM), jnp.bfloat16)
    scores = scores_of(0)
    for h in range(heads):
        following = scores_of(h + 1) if h + 1 < heads else None
        values = (left(1, h), own(2, h), right(1, h))
        total = sum(
            jnp.dot(w, jnp.concatenate([v, ones], axis=1), preferred_element_type=jnp.float32)
            for w, v in zip(weights_of(scores), values)
        )
        store(h, (total[:, :HEAD_DIM] * (1.0 / total[:, HEAD_DIM:])).astype(jnp.bfloat16))
        scores = following


def reader(refs, splits):
    def read(n, h):
        for ref, (start, stop) in zip(refs, splits):
            if start <= h < stop:
                return ref[n, :, columns((h, h + 1), start)]

    return read


def both_ways(bias_ref, q_ref, own_refs, even_refs, odd_refs, splits, store, ahead=0):
    held = reader(own_refs, splits)

    def own(n, h):
        if n:
            return held(n - 1, h)
        cols = columns((h, h + 1), -ahead)
        return q_ref[:, cols] if len(q_ref.shape) == 2 else q_ref[0, :, cols]

    first, second = reader(even_refs, splits), reader(odd_refs, splits)
    parity = lax.rem(lax.axis_index("ctx"), 2)

    @pl.when(parity == 0)
    def _():
        attend_heads(bias_ref, own, second, first, store, splits[-1][1])

    @pl.when(parity == 1)
    def _():
        attend_heads(bias_ref, own, first, second, store, splits[-1][1])


def cost(heads):
    return pl.CostEstimate(
        flops=4 * heads * 256 * 768 * HEAD_DIM,
        bytes_accessed=2 * 8 * heads * 256 * HEAD_DIM,
        transcendentals=heads * 256 * SPAN,
    )


def split_refs(refs, splits):
    n = len(splits)
    return refs[0], refs[1], refs[2 : 2 + n], refs[2 + n : 2 + 2 * n], refs[2 + 2 * n : 2 + 3 * n]


def chunk_kernel(splits, ahead, *refs):
    out_ref = refs[-1]

    def store(h, value):
        out_ref[:, columns((h, h + 1))] = value

    both_ways(*split_refs(refs, splits), splits, store, ahead)


def attend_chunk(bias, query, parts, splits, ahead=0):
    heads = splits[-1][1]
    operands = [bias, query] + [p[n] for n in range(3) for p in parts]
    return pl.pallas_call(
        functools.partial(chunk_kernel, splits, ahead),
        out_shape=jax.ShapeDtypeStruct((query.shape[0], heads * HEAD_DIM), jnp.bfloat16),
        in_specs=[VMEM] * len(operands),
        out_specs=VMEM,
        cost_estimate=cost(heads),
        compiler_params=pltpu.CompilerParams(vmem_limit_bytes=GRANT),
        name="attend",
    )(*operands)


def last_kernel(splits, spots, last, *refs):
    n = 2 + 3 * len(splits)
    heads = splits[-1][1]
    pieces, out_ref, held_ref, sems = refs[n:-3], refs[-3], refs[-2], refs[-1]
    copies = [
        pltpu.make_async_copy(piece, out_ref.at[0, :, cols], sems.at[i])
        for i, (piece, cols) in enumerate(zip(pieces, spots))
    ]
    for copy in copies:
        copy.start()
    for h in range(heads):
        cols = columns((h, h + 1))
        spot = slice(last.start + cols.start, last.start + cols.stop)
        copies.append(
            pltpu.make_async_copy(held_ref.at[:, cols], out_ref.at[0, :, spot], sems.at[len(copies)])
        )

    def store(h, value):
        held_ref[:, columns((h, h + 1))] = value
        copies[len(pieces) + h].start()

    both_ways(*split_refs(refs, splits), splits, store)
    for copy in copies:
        copy.wait()


def attend_last(bias, query, parts, splits, pieces, spots, last, shape):
    operands = [bias, query] + [p[n] for n in range(3) for p in parts] + pieces
    return pl.pallas_call(
        functools.partial(last_kernel, splits, spots, last),
        out_shape=jax.ShapeDtypeStruct(shape, jnp.bfloat16),
        in_specs=[VMEM] * len(operands),
        out_specs=pl.BlockSpec(memory_space=pl.ANY),
        scratch_shapes=[
            pltpu.VMEM((shape[1], last.stop - last.start), jnp.bfloat16),
            pltpu.SemaphoreType.DMA((len(pieces) + splits[-1][1],)),
        ],
        cost_estimate=cost(splits[-1][1]),
        compiler_params=pltpu.CompilerParams(vmem_limit_bytes=GRANT),
        name="attend_last",
    )(*operands)


def exchange(own):
    even = swap(own, 0)
    odd = swap(own, 1)
    return own, even, odd


def attention(projected, tile_mask):
    _, _, rows, width = projected.shape
    base, stop = LATE[0][0], LATE[-1][1]
    first = projected[1:, 0, :, columns(EARLY[0][0])]
    chunks = [c for group in EARLY for c in group]
    held = [first] + [projected[1:, 0, :, columns(c)] for c in chunks[1:]]
    query = projected[0, 0, :, columns((0, base))]
    parts = [exchange(own) for own in held]
    sent = projected[:, 0, :, columns((base, stop))]
    moved = lax.ppermute(sent, "pipe", ring("pipe"))
    late = [exchange(moved[1:, :, columns(c, base)]) for c in LATE]
    bias = bias_of(tile_mask)

    pieces, spots, done = [], [], 0
    for group in EARLY:
        start, end = group[0][0], group[-1][1]
        splits = tuple((a - start, b - start) for a, b in group)
        out = attend_chunk(bias, query, parts[done : done + len(group)], splits, start)
        done += len(group)
        pieces.append(lax.ppermute(out, "pipe", ring("pipe")))
        spots.append(columns((start, end)))
    for n, (c, part) in enumerate(zip(LATE, late)):
        query = moved if len(LATE) == 1 else moved[0, :, columns(c, base)]
        splits = ((0, c[1] - c[0]),)
        if n < len(LATE) - 1:
            pieces.append(attend_chunk(bias, query, [part], splits))
            spots.append(columns(c))
        else:
            return attend_last(bias, query, [part], splits, pieces, spots, columns(c), (1, rows, width))


def solution(mesh):
    placed = (P(None, "pipe", ("dp", "ctx"), None), P("ctx", None))
    return jax.shard_map(
        attention,
        mesh=mesh,
        in_specs=placed,
        out_specs=P("pipe", ("dp", "ctx"), None),
        check_vma=False,
    )
```
